32 devices in a mesh: depth: 8 (over z, y), space: 4 (over x, core).
Axes of the slice: x: 2, y: 2, z: 4, core: 2. Of those that a mesh axis runs over, the one named last changes fastest.
Arguments:
- coarse_states: float32 [8, 32, 128, 128], P('depth', 'space'), may hold values from -6 to 6
- first_kernels: bfloat16 [32, 9, 128, 128], P('depth'), may hold values from -0.1875 to 0.1875
- second_kernels: bfloat16 [32, 9, 128, 128], P('depth'), may hold values from -0.1875 to 0.1875
- coarse_channel_gain: float32 [8, 128], replicated, may hold values from 0 to 1, as said below
Outputs:
- states: float32 [32, 32, 128, 128], P('depth', 'space')
- relaxed: float32 [8, 32, 128, 128], P('depth', 'space')
The draws below stay inside these ranges and needn't reach their ends.
Inputs may be any that keep to these rules, and one draw needn't show every extreme that they name: `coarse_channel_gain`: each entry is positive and at most 1.
All inputs are finite; a program needn't handle non-finite values.
Results may differ from the reference program's by a relative error of at most 0.01.
Values may be sent and summed in bfloat16 or wider, within the bound.
A program may use at most 128 MiB of HBM per device.

```python
import jax
import jax.numpy as jnp
from jax import lax

C = 128
CF = 4
W = 128
COARSE_POINTS = 8
LAYERS = 32
H = 32


def draw_coarse_channel_gain(key, part):
    random_keys = [jax.random.fold_in(key, 101 + index) for index in range(7)]
    share = 0.5
    slow = jax.random.uniform(random_keys[0], (C,)) < share
    slow_rate = jnp.log(0.2) / COARSE_POINTS * jax.random.uniform(random_keys[1], (C,), jnp.float32, 0.3, 1.0)
    fast_rate = jnp.log(0.1) / jax.random.uniform(random_keys[2], (C,), jnp.float32, 4.0, 20.0)
    rate = jnp.where(slow, slow_rate, fast_rate)
    jitter = jax.random.uniform(random_keys[3], (COARSE_POINTS, 1), jnp.float32, 0.5, 1.5)
    relaxation_sweep = jax.random.uniform(random_keys[4], (COARSE_POINTS, 1)) < 3.0 / COARSE_POINTS
    multiplier = jnp.where(relaxation_sweep, jax.random.uniform(random_keys[5], (COARSE_POINTS, 1), jnp.float32, 0.5, 0.8), 1.0)
    return (jnp.exp(rate[None, :] * jitter) * multiplier).astype(jnp.float32)


def shard_levels(stream_key, extent, shards, low, high):
    loudness, own = 1.0, jax.random.fold_in(stream_key, 6)
    for axis_at, blocks in shards:
        heights = jnp.exp(jax.random.uniform(jax.random.fold_in(own, axis_at), (blocks,), jnp.float32, low / len(shards), high / len(shards)))
        loudness = loudness * jnp.repeat(heights, extent[axis_at] // blocks).reshape([-1 if axis == axis_at else 1 for axis in range(len(extent))])
    return loudness


def gaussian(stream_key, extent, scale, most, cuts=(), kind=jnp.bfloat16):
    values = jax.random.normal(stream_key, extent, jnp.float32) * scale
    if len(cuts) > 0:
        values = shard_levels(stream_key, extent, cuts, -0.22, 0.18) * values
    return jnp.clip(values, min=-most, max=most).astype(kind)


def setup_inputs(seed: int = 0) -> dict:
    streams_of = jax.random.split(jax.random.key(seed), 5)
    return {
        "coarse_states": gaussian(streams_of[0], (COARSE_POINTS, H, W, C), 1.0, 6.0, ((0, 8), (1, 4)), jnp.float32),
        "first_kernels": gaussian(streams_of[1], (LAYERS, 9, C, C), (9 * C) ** -0.5, 0.1875, ((0, 8),)),
        "second_kernels": gaussian(streams_of[2], (LAYERS, 9, C, C), (9 * C) ** -0.5, 0.1875, ((0, 8),)),
        "coarse_channel_gain": draw_coarse_channel_gain(jax.random.fold_in(streams_of[4], 71), 0),
    }


def conv_taps(padded, kernel):
    rows = padded.shape[0] - 2
    cols = padded.shape[1]
    wide = jnp.pad(padded, ((0, 0), (1, 1), (0, 0)))
    parts = [wide[a:a + rows, b:b + cols, :] for a in range(3) for b in range(3)]
    stacked = jnp.concatenate(parts, axis=-1).reshape(rows * cols, -1)
    flat = kernel.reshape(-1, kernel.shape[-1])
    return jnp.dot(stacked, flat, preferred_element_type=jnp.float32).reshape(rows, cols, -1)


def layer_step(state, first, second_half):
    inner = jnp.pad(state.astype(jnp.bfloat16), ((1, 1), (0, 0), (0, 0)))
    hidden = jnp.tanh(conv_taps(inner, first)).astype(jnp.bfloat16)
    outer = conv_taps(jnp.pad(hidden, ((1, 1), (0, 0), (0, 0))), second_half)
    return state + 0.5 * jnp.tanh(outer)


def propagate(start, firsts, seconds):
    state = start
    for index in range(CF):
        state = layer_step(state, firsts[index], seconds[index])
    return state


def reference(coarse_states, first_kernels, second_kernels, coarse_channel_gain):
    firsts = first_kernels.reshape(COARSE_POINTS, CF, 9, C, C)
    seconds = second_kernels.reshape(COARSE_POINTS, CF, 9, C, C)

    def sweep_all(starts):
        return lax.map(lambda args: propagate(args[0], args[1], args[2]), (starts, firsts, seconds))

    y_first = sweep_all(coarse_states)
    c_first = jnp.concatenate([coarse_states[:1], y_first[:-1]], axis=0)
    y_second = sweep_all(c_first)
    resid = jnp.concatenate([jnp.zeros_like(c_first[:1]), y_second[:-1] - c_first[1:]], axis=0)

    def chain(carry, pair):
        gain, term = pair
        nxt = gain * carry + term
        return nxt, nxt

    zero_state = jnp.zeros(coarse_states.shape[1:], jnp.float32)
    _, errors = lax.scan(chain, zero_state, (coarse_channel_gain, resid))
    c_second = c_first + errors

    def points(args):
        state, fk, sk = args
        listing = [state]
        for index in range(CF - 1):
            state = layer_step(state, fk[index], sk[index])
            listing.append(state)
        return jnp.stack(listing, axis=0)

    result = lax.map(points, (c_second, firsts, seconds))
    return result.reshape(LAYERS, H, W, C), y_second
```

```python
import functools

import jax
import jax.numpy as jnp
from jax import lax
from jax.experimental import pallas as pl
from jax.experimental.pallas import tpu as pltpu
from jax.sharding import PartitionSpec as P

MESH = pl.DeviceIdType.MESH
F32 = jnp.float32
BF16 = jnp.bfloat16


def conv_pairs(row, starts, taps):
    lhs = jnp.concatenate(
        [jnp.concatenate([row(s + i) for s in starts], axis=0) for i in range(4)], axis=1
    )
    count = lhs.shape[0]
    cols = count // len(starts)
    parts = []
    for b in range(3):
        top, mid, low = (taps(3 * a + b) for a in range(3))
        none = jnp.zeros_like(top)
        weight = jnp.concatenate(
            [
                jnp.concatenate([top, none], axis=1),
                jnp.concatenate([mid, top], axis=1),
                jnp.concatenate([low, mid], axis=1),
                jnp.concatenate([none, low], axis=1),
            ],
            axis=0,
        )
        parts.append(jnp.dot(lhs, weight, preferred_element_type=F32))
    column = lax.broadcasted_iota(jnp.int32, parts[0].shape, 0) % cols
    left = jnp.where(column == 0, 0.0, pltpu.roll(parts[0], 1, 0))
    right = jnp.where(column == cols - 1, 0.0, pltpu.roll(parts[2], count - 1, 0))
    return parts[1] + left + right


def cycle_kernel(
    depths,
    spaces,
    start_ref,
    first_ref,
    second_ref,
    gain_ref,
    states_ref,
    relaxed_ref,
    xbuf,
    hbuf,
    sbuf,
    ybuf,
    cbuf,
    qsend,
    qrecv,
    tsend,
    trecv,
    fsend,
    frecv,
    halo_send,
    halo_recv,
    y_send,
    y_recv,
    scan_send,
    scan_recv,
    out_sem,
    relaxed_sem,
):
    layers = first_ref.shape[0]
    rows, cols, chans = start_ref.shape
    half = rows // 2
    d = lax.axis_index("depth")
    s = lax.axis_index("space")
    odd = d % 2
    partner = d + 1 - 2 * odd

    barrier = pltpu.get_barrier_semaphore()

    meets = [
        (s > 0, (d, s - 1)),
        (s < spaces - 1, (d, s + 1)),
        (d > 0, (d - 1, s)),
        (d < depths - 1, (d + 1, s)),
        (d > 1, (d - 2, s)),
        (d < depths - 2, (d + 2, s)),
    ]
    def greet(there, device):
        @pl.when(there)
        def _():
            pl.semaphore_signal(barrier, inc=1, device_id=device, device_id_type=MESH)

    for there, device in meets:
        greet(there, device)
    pl.semaphore_wait(barrier, sum(there.astype(jnp.int32) for there, _ in meets))

    def halo_up(slot):
        return pltpu.make_async_remote_copy(
            src_ref=xbuf.at[slot, pl.ds(2, 2)],
            dst_ref=xbuf.at[slot, pl.ds(rows + 2, 2)],
            send_sem=halo_send.at[slot, 0],
            recv_sem=halo_recv.at[slot, 0],
            device_id=(d, s - 1),
            device_id_type=MESH,
        )

    def halo_down(slot):
        return pltpu.make_async_remote_copy(
            src_ref=xbuf.at[slot, pl.ds(rows, 2)],
            dst_ref=xbuf.at[slot, pl.ds(0, 2)],
            send_sem=halo_send.at[slot, 1],
            recv_sem=halo_recv.at[slot, 1],
            device_id=(d, s + 1),
            device_id_type=MESH,
        )

    def halo_start(slot):
        @pl.when(s > 0)
        def _():
            halo_up(slot).start()

        @pl.when(s < spaces - 1)
        def _():
            halo_down(slot).start()

    def halo_wait(slot):
        @pl.when(s < spaces - 1)
        def _():
            halo_up(slot).wait_recv()
            halo_down(slot).wait_send()

        @pl.when(s > 0)
        def _():
            halo_down(slot).wait_recv()
            halo_up(slot).wait_send()

    def layer(index, slot, src, dst, keep):
        def hidden_rows(starts):
            out = conv_pairs(lambda r: xbuf[slot, r], starts, lambda k: first_ref[index, k])
            out = jnp.tanh(out).astype(BF16)
            for n, r in enumerate(starts):
                hbuf[r] = out[n * cols : (n + 1) * cols, :chans]
                hbuf[r + 1] = out[n * cols : (n + 1) * cols, chans:]

        def state_rows(starts):
            out = conv_pairs(lambda r: hbuf[r], starts, lambda k: second_ref[index, k])
            out = 0.5 * jnp.tanh(out)
            for n, r in enumerate(starts):
                for i in range(2):
                    new = sbuf[src, r + i] + out[n * cols : (n + 1) * cols, i * chans : (i + 1) * chans]
                    sbuf[dst, r + i] = new
                    xbuf[1 - slot, r + i + 2] = new.astype(BF16)

        hidden_rows(range(2, rows, 2))
        state_rows(range(2, rows - 2, 2))
        halo_wait(slot)
        hidden_rows((0, rows))

        @pl.when(s == 0)
        def _():
            hbuf[0] = jnp.zeros_like(hbuf[0])

        @pl.when(s == spaces - 1)
        def _():
            hbuf[rows + 1] = jnp.zeros_like(hbuf[rows + 1])

        state_rows((0, rows - 2))

        @pl.when(keep)
        def _():
            halo_start(1 - slot)

    @pl.when(s == 0)
    def _():
        for slot in range(2):
            xbuf[slot, pl.ds(0, 2)] = jnp.zeros((2, cols, chans), BF16)

    @pl.when(s == spaces - 1)
    def _():
        for slot in range(2):
            xbuf[slot, pl.ds(rows + 2, 2)] = jnp.zeros((2, cols, chans), BF16)

    def begin(slot, source):
        xbuf[slot, pl.ds(2, rows)] = sbuf[source].astype(BF16)
        halo_start(slot)

    sbuf[layers] = start_ref[...]
    begin(0, layers)

    def first_sweep(i, carry):
        layer(i, i % 2, layers, layers, i < layers - 1)
        return carry

    lax.fori_loop(0, layers, first_sweep, 0)

    y_copy = pltpu.make_async_remote_copy(
        src_ref=ybuf,
        dst_ref=cbuf,
        send_sem=y_send,
        recv_sem=y_recv,
        device_id=(d + 1, s),
        device_id_type=MESH,
    )
    ybuf[...] = sbuf[layers].astype(BF16)

    @pl.when(d < depths - 1)
    def _():
        y_copy.start()

    @pl.when(d == 0)
    def _():
        sbuf[0] = start_ref[...]

    @pl.when(d > 0)
    def _():
        y_copy.wait_recv()
        sbuf[0] = cbuf[...].astype(F32)

    begin(layers % 2, 0)

    def second_sweep(i, carry):
        layer(i, (layers + i) % 2, layers * ((i + layers - 1) // layers), layers, i < layers - 1)
        return carry

    lax.fori_loop(0, layers, second_sweep, 0)

    relaxed_copy = pltpu.make_async_copy(sbuf.at[layers], relaxed_ref.at[0], relaxed_sem)
    relaxed_copy.start()

    def scan_copy(kind, r, src, dst, device):
        return pltpu.make_async_remote_copy(
            src_ref=src.at[r],
            dst_ref=dst.at[r],
            send_sem=scan_send.at[kind, r],
            recv_sem=scan_recv.at[kind, r],
            device_id=(device, s),
            device_id_type=MESH,
        )

    mine = odd * half
    theirs = half - mine
    for r in range(half):
        qsend[r] = (sbuf[layers, theirs + r] - ybuf[theirs + r].astype(F32)).astype(BF16)
        scan_copy(0, r, qsend, qrecv, partner).start()

    even = d - odd
    gain_odd = gain_ref[pl.ds((even + 1) % depths, 1), :]
    gain_next = gain_ref[pl.ds((even + 2) % depths, 1), :]

    @pl.when(d < 2)
    def _():
        trecv[...] = jnp.zeros_like(trecv)

    for r in range(half):
        own = sbuf[layers, mine + r] - ybuf[mine + r].astype(F32)
        scan_copy(0, r, qsend, qrecv, partner).wait_recv()
        other = qrecv[r].astype(F32)
        q_even = jnp.where(odd == 0, own, other)
        q_odd = jnp.where(odd == 0, other, own)

        @pl.when(d > 1)
        def _():
            scan_copy(1, r, tsend, trecv, d + 2).wait_recv()

        e_even = trecv[r].astype(F32)
        e_odd = gain_odd * e_even + q_even

        @pl.when(d < depths - 2)
        def _():
            tsend[r] = (gain_next * e_odd + q_odd).astype(BF16)
            scan_copy(1, r, tsend, trecv, d + 2).start()

        fsend[r] = jnp.where(odd == 0, e_odd, e_even).astype(BF16)
        scan_copy(2, r, fsend, frecv, partner).start()
        sbuf[0, mine + r] = sbuf[0, mine + r] + jnp.where(odd == 0, e_even, e_odd)

    for r in range(half):
        scan_copy(2, r, fsend, frecv, partner).wait_recv()
        sbuf[0, theirs + r] = sbuf[0, theirs + r] + frecv[r].astype(F32)

    begin((2 * layers) % 2, 0)

    def out_copy(i):
        return pltpu.make_async_copy(sbuf.at[i], states_ref.at[i], out_sem.at[i])

    out_copy(0).start()

    def third_sweep(i, carry):
        layer(i, i % 2, i, i + 1, i < layers - 2)
        out_copy(i + 1).start()
        return carry

    lax.fori_loop(0, layers - 1, third_sweep, 0)

    @pl.when(d < depths - 1)
    def _():
        y_copy.wait_send()

    for r in range(half):
        scan_copy(0, r, qsend, qrecv, partner).wait_send()
        scan_copy(2, r, fsend, frecv, partner).wait_send()

        @pl.when(d < depths - 2)
        def _():
            scan_copy(1, r, tsend, trecv, d + 2).wait_send()

    relaxed_copy.wait()
    for i in range(layers):
        out_copy(i).wait()


def shards(depths, spaces, coarse_states, first_kernels, second_kernels, coarse_channel_gain):
    layers, taps, chans, _ = first_kernels.shape
    _, rows, cols, _ = coarse_states.shape
    half = rows // 2
    vmem = pl.BlockSpec(memory_space=pltpu.VMEM)
    hbm = pl.BlockSpec(memory_space=pl.ANY)
    part = pltpu.VMEM((half, cols, chans), BF16)
    return pl.pallas_call(
        functools.partial(cycle_kernel, depths, spaces),
        out_shape=(
            jax.ShapeDtypeStruct((layers, rows, cols, chans), F32),
            jax.ShapeDtypeStruct((1, rows, cols, chans), F32),
        ),
        in_specs=[vmem] * 4,
        out_specs=(hbm, hbm),
        scratch_shapes=[
            pltpu.VMEM((2, rows + 4, cols, chans), BF16),
            pltpu.VMEM((rows + 2, cols, chans), BF16),
            pltpu.VMEM((layers + 1, rows, cols, chans), F32),
            pltpu.VMEM((rows, cols, chans), BF16),
            pltpu.VMEM((rows, cols, chans), BF16),
            part,
            part,
            part,
            part,
            part,
            part,
            pltpu.SemaphoreType.DMA((2, 2)),
            pltpu.SemaphoreType.DMA((2, 2)),
            pltpu.SemaphoreType.DMA,
            pltpu.SemaphoreType.DMA,
            pltpu.SemaphoreType.DMA((3, half)),
            pltpu.SemaphoreType.DMA((3, half)),
            pltpu.SemaphoreType.DMA((layers,)),
            pltpu.SemaphoreType.DMA,
        ],
        compiler_params=pltpu.CompilerParams(
            collective_id=0, has_side_effects=True, vmem_limit_bytes=56 * 1024 * 1024
        ),
    )(coarse_states[0], first_kernels, second_kernels, coarse_channel_gain)


def solution(mesh):
    depths, spaces = mesh.shape["depth"], mesh.shape["space"]
    placed = (
        P("depth", "space", None, None),
        P("depth", None, None, None),
        P("depth", None, None, None),
        P(),
    )
    return jax.shard_map(
        functools.partial(shards, depths, spaces),
        mesh=mesh,
        in_specs=placed,
        out_specs=(P("depth", "space", None, None), P("depth", "space", None, None)),
        check_vma=False,
    )
```

```python
import functools

import jax
import jax.numpy as jnp
from jax import lax
from jax.experimental import pallas as pl
from jax.experimental.pallas import tpu as pltpu
from jax.sharding import PartitionSpec as P

MESH = pl.DeviceIdType.MESH
F32 = jnp.float32
BF16 = jnp.bfloat16


def conv_pairs(row, starts, taps):
    lhs = jnp.concatenate(
        [jnp.concatenate([row(s + i) for s in starts], axis=0) for i in range(4)], axis=1
    )
    count = lhs.shape[0]
    cols = count // len(starts)
    parts = []
    for b in range(3):
        top, mid, low = (taps(3 * a + b) for a in range(3))
        none = jnp.zeros_like(top)
        weight = jnp.concatenate(
            [
                jnp.concatenate([top, none], axis=1),
                jnp.concatenate([mid, top], axis=1),
                jnp.concatenate([low, mid], axis=1),
                jnp.concatenate([none, low], axis=1),
            ],
            axis=0,
        )
        parts.append(jnp.dot(lhs, weight, preferred_element_type=F32))
    column = lax.broadcasted_iota(jnp.int32, parts[0].shape, 0) % cols
    left = jnp.where(column == 0, 0.0, pltpu.roll(parts[0], 1, 0))
    right = jnp.where(column == cols - 1, 0.0, pltpu.roll(parts[2], count - 1, 0))
    return parts[1] + left + right


def cycle_kernel(
    depths,
    spaces,
    start_ref,
    first_ref,
    second_ref,
    gain_ref,
    states_ref,
    relaxed_ref,
    xbuf,
    hbuf,
    sbuf,
    ybuf,
    cbuf,
    qsend,
    qrecv,
    tsend,
    trecv,
    fsend,
    frecv,
    halo_send,
    halo_recv,
    y_send,
    y_recv,
    scan_send,
    scan_recv,
    out_sem,
    relaxed_sem,
):
    layers = first_ref.shape[0]
    rows, cols, chans = start_ref.shape
    half = rows // 2
    d = lax.axis_index("depth")
    s = lax.axis_index("space")
    odd = d % 2
    partner = d + 1 - 2 * odd

    barrier = pltpu.get_barrier_semaphore()

    meets = [
        (s > 0, (d, s - 1)),
        (s < spaces - 1, (d, s + 1)),
        (d > 0, (d - 1, s)),
        (d < depths - 1, (d + 1, s)),
        (d > 1, (d - 2, s)),
        (d < depths - 2, (d + 2, s)),
    ]
    def greet(there, device):
        @pl.when(there)
        def _():
            pl.semaphore_signal(barrier, inc=1, device_id=device, device_id_type=MESH)

    for there, device in meets:
        greet(there, device)
    pl.semaphore_wait(barrier, sum(there.astype(jnp.int32) for there, _ in meets))

    def halo_up(slot):
        return pltpu.make_async_remote_copy(
            src_ref=xbuf.at[slot, pl.ds(2, 2)],
            dst_ref=xbuf.at[slot, pl.ds(rows + 2, 2)],
            send_sem=halo_send.at[slot, 0],
            recv_sem=halo_recv.at[slot, 0],
            device_id=(d, s - 1),
            device_id_type=MESH,
        )

    def halo_down(slot):
        return pltpu.make_async_remote_copy(
            src_ref=xbuf.at[slot, pl.ds(rows, 2)],
            dst_ref=xbuf.at[slot, pl.ds(0, 2)],
            send_sem=halo_send.at[slot, 1],
            recv_sem=halo_recv.at[slot, 1],
            device_id=(d, s + 1),
            device_id_type=MESH,
        )

    def halo_start(slot, side):
        @pl.when((side == 0) & (s > 0))
        def _():
            halo_up(slot).start()

        @pl.when((side == 1) & (s < spaces - 1))
        def _():
            halo_down(slot).start()

    def halo_wait(slot, side):
        @pl.when((side == 0) & (s > 0))
        def _():
            halo_down(slot).wait_recv()
            halo_up(slot).wait_send()

        @pl.when((side == 1) & (s < spaces - 1))
        def _():
            halo_up(slot).wait_recv()
            halo_down(slot).wait_send()

    last_side = s % 2

    def layer(index, slot, src, dst, keep, inner_done, edge_done):
        def hidden_rows(starts, side=None):
            out = conv_pairs(lambda r: xbuf[slot, r], starts, lambda k: first_ref[index, k])
            out = jnp.tanh(out).astype(BF16)
            for n, r in enumerate(starts):
                one = out[n * cols : (n + 1) * cols, :chans]
                two = out[n * cols : (n + 1) * cols, chans:]
                if side is not None:
                    one = jnp.where((side == 0) & (s == 0), jnp.zeros_like(one), one)
                    two = jnp.where((side == 1) & (s == spaces - 1), jnp.zeros_like(two), two)
                hbuf[r] = one
                hbuf[r + 1] = two

        def state_rows(starts):
            out = conv_pairs(lambda r: hbuf[r], starts, lambda k: second_ref[index, k])
            out = 0.5 * jnp.tanh(out)
            for n, r in enumerate(starts):
                for i in range(2):
                    new = sbuf[src, r + i] + out[n * cols : (n + 1) * cols, i * chans : (i + 1) * chans]
                    sbuf[dst, r + i] = new
                    xbuf[1 - slot, r + i + 2] = new.astype(BF16)

        hidden_rows(range(2, rows, 2))
        state_rows(range(2, rows - 2, 2))
        inner_done()
        for side in (1 - last_side, last_side):
            halo_wait(slot, side)
            hidden_rows((side * rows,), side)
            state_rows((side * (rows - 2),))

            @pl.when(keep)
            def _():
                halo_start(1 - slot, side)

            edge_done(side)

    @pl.when(s == 0)
    def _():
        for slot in range(2):
            xbuf[slot, pl.ds(0, 2)] = jnp.zeros((2, cols, chans), BF16)

    @pl.when(s == spaces - 1)
    def _():
        for slot in range(2):
            xbuf[slot, pl.ds(rows + 2, 2)] = jnp.zeros((2, cols, chans), BF16)

    def begin(slot, source):
        xbuf[slot, pl.ds(2, rows)] = sbuf[source].astype(BF16)
        for side in range(2):
            halo_start(slot, side)

    sbuf[layers] = start_ref[...]
    begin(0, layers)

    def y_copy(first, count, k):
        return pltpu.make_async_remote_copy(
            src_ref=ybuf.at[pl.ds(first, count)],
            dst_ref=cbuf.at[pl.ds(first, count)],
            send_sem=y_send.at[k],
            recv_sem=y_recv.at[k],
            device_id=(d + 1, s),
            device_id_type=MESH,
        )

    y_parts = ((2, rows - 4, 2), (0, 2, 0), (rows - 2, 2, 1))

    def y_out(first, count, k, slot):
        ybuf[pl.ds(first, count)] = xbuf[1 - slot, pl.ds(first + 2, count)]

        @pl.when(d < depths - 1)
        def _():
            y_copy(first, count, k).start()

    def first_sweep(i, carry):
        slot = i % 2

        def inner_done():
            @pl.when(i == layers - 1)
            def _():
                y_out(2, rows - 4, 2, slot)

        def edge_done(side):
            @pl.when(i == layers - 1)
            def _():
                y_out(side * (rows - 2), 2, side, slot)

        layer(i, slot, layers, layers, i < layers - 1, inner_done, edge_done)
        return carry

    lax.fori_loop(0, layers, first_sweep, 0)

    @pl.when(d == 0)
    def _():
        sbuf[0] = start_ref[...]

    @pl.when(d > 0)
    def _():
        for first, count, k in y_parts:
            y_copy(first, count, k).wait_recv()
            sbuf[0, pl.ds(first, count)] = cbuf[pl.ds(first, count)].astype(F32)

    begin(layers % 2, 0)

    part = cols // 2
    mine = odd * half
    theirs = half - mine

    def scan_copy(kind, r, h, src, dst, device):
        return pltpu.make_async_remote_copy(
            src_ref=src.at[r, pl.ds(h * part, part)],
            dst_ref=dst.at[r, pl.ds(h * part, part)],
            send_sem=scan_send.at[kind, r, h],
            recv_sem=scan_recv.at[kind, r, h],
            device_id=(device, s),
            device_id_type=MESH,
        )

    def q_out(first, count):
        for k in range(count):
            r = first + k
            qsend[r] = (sbuf[layers, theirs + r] - ybuf[theirs + r].astype(F32)).astype(BF16)
            for h in range(2):
                scan_copy(0, r, h, qsend, qrecv, partner).start()

    def second_sweep(i, carry):
        def inner_done():
            @pl.when(i == layers - 1)
            def _():
                q_out(2 * odd, half - 2)

        def edge_done(side):
            @pl.when((i == layers - 1) & (side == 1 - odd))
            def _():
                q_out((1 - odd) * (half - 2), 2)

        layer(
            i,
            (layers + i) % 2,
            layers * ((i + layers - 1) // layers),
            layers,
            i < layers - 1,
            inner_done,
            edge_done,
        )
        return carry

    lax.fori_loop(0, layers, second_sweep, 0)

    relaxed_copy = pltpu.make_async_copy(sbuf.at[layers], relaxed_ref.at[0], relaxed_sem)
    relaxed_copy.start()

    even = d - odd
    gain_odd = gain_ref[pl.ds((even + 1) % depths, 1), :]
    gain_next = gain_ref[pl.ds((even + 2) % depths, 1), :]

    @pl.when(d < 2)
    def _():
        trecv[...] = jnp.zeros_like(trecv)

    order = [((k + (1 - odd) * 2) % half, h) for k in range(half) for h in range(2)]
    for r, h in order:
        piece = pl.ds(h * part, part)
        own = sbuf[layers, mine + r, piece] - ybuf[mine + r, piece].astype(F32)
        scan_copy(0, r, h, qsend, qrecv, partner).wait_recv()
        other = qrecv[r, piece].astype(F32)
        q_even = jnp.where(odd == 0, own, other)
        q_odd = jnp.where(odd == 0, other, own)

        @pl.when(d > 1)
        def _():
            scan_copy(1, r, h, tsend, trecv, d + 2).wait_recv()

        e_even = trecv[r, piece].astype(F32)
        e_odd = gain_odd * e_even + q_even

        @pl.when(d < depths - 2)
        def _():
            tsend[r, piece] = (gain_next * e_odd + q_odd).astype(BF16)
            scan_copy(1, r, h, tsend, trecv, d + 2).start()

        fsend[r, piece] = jnp.where(odd == 0, e_odd, e_even).astype(BF16)
        scan_copy(2, r, h, fsend, frecv, partner).start()
        sbuf[0, mine + r, piece] = sbuf[0, mine + r, piece] + jnp.where(odd == 0, e_even, e_odd)

    for k in range(half):
        r = (k + odd * 2) % half
        for h in range(2):
            scan_copy(2, r, h, fsend, frecv, partner).wait_recv()
        sbuf[0, theirs + r] = sbuf[0, theirs + r] + frecv[r].astype(F32)

    begin((2 * layers) % 2, 0)

    def out_copy(i):
        return pltpu.make_async_copy(sbuf.at[i], states_ref.at[i], out_sem.at[i])

    out_copy(0).start()

    def third_sweep(i, carry):
        layer(i, i % 2, i, i + 1, i < layers - 2, lambda: None, lambda side: None)
        out_copy(i + 1).start()
        return carry

    lax.fori_loop(0, layers - 1, third_sweep, 0)

    @pl.when(d < depths - 1)
    def _():
        for first, count, k in y_parts:
            y_copy(first, count, k).wait_send()

    for r in range(half):
        for h in range(2):
            scan_copy(0, r, h, qsend, qrecv, partner).wait_send()
            scan_copy(2, r, h, fsend, frecv, partner).wait_send()

            @pl.when(d < depths - 2)
            def _():
                scan_copy(1, r, h, tsend, trecv, d + 2).wait_send()

    relaxed_copy.wait()
    for i in range(layers):
        out_copy(i).wait()


def shards(depths, spaces, coarse_states, first_kernels, second_kernels, coarse_channel_gain):
    layers, taps, chans, _ = first_kernels.shape
    _, rows, cols, _ = coarse_states.shape
    half = rows // 2
    vmem = pl.BlockSpec(memory_space=pltpu.VMEM)
    hbm = pl.BlockSpec(memory_space=pl.ANY)
    part = pltpu.VMEM((half, cols, chans), BF16)
    return pl.pallas_call(
        functools.partial(cycle_kernel, depths, spaces),
        out_shape=(
            jax.ShapeDtypeStruct((layers, rows, cols, chans), F32),
            jax.ShapeDtypeStruct((1, rows, cols, chans), F32),
        ),
        in_specs=[vmem] * 4,
        out_specs=(hbm, hbm),
        scratch_shapes=[
            pltpu.VMEM((2, rows + 4, cols, chans), BF16),
            pltpu.VMEM((rows + 2, cols, chans), BF16),
            pltpu.VMEM((layers + 1, rows, cols, chans), F32),
            pltpu.VMEM((rows, cols, chans), BF16),
            pltpu.VMEM((rows, cols, chans), BF16),
            part,
            part,
            part,
            part,
            part,
            part,
            pltpu.SemaphoreType.DMA((2, 2)),
            pltpu.SemaphoreType.DMA((2, 2)),
            pltpu.SemaphoreType.DMA((3,)),
            pltpu.SemaphoreType.DMA((3,)),
            pltpu.SemaphoreType.DMA((3, half, 2)),
            pltpu.SemaphoreType.DMA((3, half, 2)),
            pltpu.SemaphoreType.DMA((layers,)),
            pltpu.SemaphoreType.DMA,
        ],
        compiler_params=pltpu.CompilerParams(
            collective_id=0, has_side_effects=True, vmem_limit_bytes=24 * 1024 * 1024
        ),
    )(coarse_states[0], first_kernels, second_kernels, coarse_channel_gain)


def solution(mesh):
    depths, spaces = mesh.shape["depth"], mesh.shape["space"]
    placed = (
        P("depth", "space", None, None),
        P("depth", None, None, None),
        P("depth", None, None, None),
        P(),
    )
    return jax.shard_map(
        functools.partial(shards, depths, spaces),
        mesh=mesh,
        in_specs=placed,
        out_specs=(P("depth", "space", None, None), P("depth", "space", None, None)),
        check_vma=False,
    )
```
